32 devices in a mesh: dp: 4 (over y, x), mp: 8 (over z, core).
Axes of the slice: x: 2, y: 2, z: 4, core: 2. Of those that a mesh axis runs over, the one named last changes fastest.
Arguments:
- tokens: bfloat16 [8192, 2048], P(('dp', 'mp')), may hold values from -6 to 6
- ln1_gain: float32 [2048], replicated, may hold values from 0.5 to 1.5
- ln1_bias: float32 [2048], replicated, may hold values from -1.75 to 1.75
- w_query: bfloat16 [2048, 2048], P(None, 'mp'), may hold values from -0.125 to 0.125
- b_query: float32 [2048], P('mp'), may hold values from -3 to 3
- w_key: bfloat16 [2048, 2048], P(None, 'mp'), may hold values from -0.125 to 0.125
- w_value: bfloat16 [2048, 2048], P(None, 'mp'), may hold values from -0.125 to 0.125
- b_value: float32 [2048], P('mp'), may hold values from -0.125 to 0.125
- w_out: bfloat16 [2048, 2048], P('mp'), may hold values from -2 to 2
- b_out: float32 [2048], replicated, may hold values from -3 to 3
- ln2_gain: float32 [2048], replicated, may hold values from 0.5 to 1.5
- ln2_bias: float32 [2048], replicated, may hold values from -1.75 to 1.75
- w_up: bfloat16 [2048, 8192], P(None, 'mp'), may hold values from -0.125 to 0.125
- b_up: float32 [8192], P('mp'), may hold values from -3 to 3
- w_down: bfloat16 [8192, 2048], P('mp'), may hold values from -0.0625 to 0.0625
- b_down: float32 [2048], replicated, may hold values from -3 to 3
- cotangent: bfloat16 [8192, 2048], P(('dp', 'mp')), may hold values from -6 to 6
- seq_ids: int32 [4, 2048], P('dp'), may hold values from 0 to 2, as said below
- block_mask: int32 [4, 8, 8], P('dp'), may hold values from 0 to 1, as said below
- counts: int32 [4], replicated, may hold values from 512 to 2048, as said below
Outputs:
- output: float32 [8192, 2048], P(('dp', 'mp'))
- grad_in: float32 [8192, 2048], P(('dp', 'mp'))
- grad_ln1_gain: float32 [2048], replicated
- grad_ln1_bias: float32 [2048], replicated
- grad_w_query: float32 [2048, 2048], P(None, 'mp')
- grad_b_query: float32 [2048], P('mp')
- grad_w_key: float32 [2048, 2048], P(None, 'mp')
- grad_w_value: float32 [2048, 2048], P(None, 'mp')
- grad_b_value: float32 [2048], P('mp')
- grad_w_out: float32 [2048, 2048], P('mp')
- grad_b_out: float32 [2048], replicated
- grad_ln2_gain: float32 [2048], replicated
- grad_ln2_bias: float32 [2048], replicated
- grad_w_up: float32 [2048, 8192], P(None, 'mp')
- grad_b_up: float32 [8192], P('mp')
- grad_w_down: float32 [8192, 2048], P('mp')
- grad_b_down: float32 [2048], replicated
The draws below stay inside these ranges and needn't reach their ends.
Inputs may be any that keep to these rules, and one draw needn't show every extreme that they name: `counts`: one group's count equals 2048 in every draw. `seq_ids`: in group g, slots before a cut carry 0, slots from the cut up to counts[g] - 1 carry 1, later slots carry 2; the cut lies between max(counts[g] - 2048, counts[g] // 2) and min(counts[g], 2048). `block_mask`: diagonal entries are 1 and entries above the diagonal are 0.
All inputs are finite; a program needn't handle non-finite values.
Results may differ from the reference program's by a relative error of at most 0.012.
Values may be sent and summed in bfloat16 or wider, within the bound.
No kernel may reach another device: no remote copies, remote signals or barrier semaphores. Data moves between devices by JAX's collectives and lax.ppermute only.
A program may use at most 256 MiB of HBM per device.

```python
import jax
import jax.numpy as jnp
from jax import lax

D = 2048
HEADS = 16
HD = 128
FF = 8192
BLOCK = 256
TOK_GROUP = 2048
TOKENS = 8192
N_DP = 4


def group_layout(key):
    base_key = jax.random.fold_in(key, 11)
    first_key, second_key, third_key = jax.random.split(base_key, 3)
    counts = jax.random.randint(first_key, (N_DP,), TOK_GROUP // 4, TOK_GROUP + 1)
    fullest = jax.random.randint(second_key, (), 0, N_DP)
    counts = jnp.where(jnp.arange(N_DP) == fullest, TOK_GROUP, counts).astype(jnp.int32)
    fraction = jax.random.randint(third_key, (N_DP,), 0, 1025)
    lowest = jnp.maximum(counts - 2048, counts // 2)
    highest_cut = jnp.minimum(counts, 2048)
    cut_points = lowest + (highest_cut - lowest) * fraction // 1024
    return (counts, cut_points.astype(jnp.int32))


def draw_counts(key, part):
    return group_layout(key)[0]


def draw_seq_ids(key, part):
    counts, cut_points = group_layout(key)
    positions = jnp.arange(TOK_GROUP, dtype=jnp.int32)[None, :]
    inside = jnp.where(positions < counts[:, None], 1, 2)
    return jnp.where(positions < cut_points[:, None], 0, inside).astype(jnp.int32)


def draw_block_mask(key, part):
    blocks = TOK_GROUP // BLOCK
    coin_flips = jax.random.randint(jax.random.fold_in(key, 23), (N_DP, blocks, blocks), 0, 2)
    block_rows = jnp.arange(blocks)[:, None]
    block_cols = jnp.arange(blocks)[None, :]
    below = jnp.where(block_cols < block_rows, coin_flips, 0)
    return jnp.where(block_cols == block_rows, 1, below).astype(jnp.int32)


def level_of(key, dims, cuts, low, top_value):
    factor_of = 1.0
    for axis_at, parts in cuts:
        heights = jax.random.uniform(jax.random.fold_in(jax.random.fold_in(key, 6), axis_at), (parts,), jnp.float32, low / len(cuts), top_value / len(cuts))
        factor_of = factor_of * jnp.repeat(jnp.exp(heights), dims[axis_at] // parts).reshape((-1,) + (1,) * (len(dims) - 1 - axis_at))
    return factor_of


def noise(stream_key, extent, scale, limit, pieces=(), kind=jnp.bfloat16):
    level = level_of(stream_key, extent, pieces, -0.22, 0.18) if pieces else 1.0
    values = jax.random.normal(stream_key, extent, jnp.float32) * scale * level
    return jnp.minimum(jnp.maximum(values, -limit), limit).astype(kind)


def setup_inputs(seed: int = 0) -> dict:
    keys = jax.random.split(jax.random.key(seed), 21)
    return {
        "tokens": noise(keys[0], (TOKENS, D), 1.0, 6.0, ((0, 32),)),
        "ln1_gain": jnp.clip(1.0 + 0.1 * jax.random.normal(keys[1], (D,), jnp.float32), 0.5, 1.5),
        "ln1_bias": noise(keys[2], (D,), 0.3, 1.75, (), jnp.float32),
        "w_query": noise(keys[3], (D, D), D ** -0.5, 0.125, ((1, 8),)),
        "b_query": noise(keys[4], (D,), 0.5, 3.0, ((0, 8),), jnp.float32),
        "w_key": noise(keys[5], (D, D), D ** -0.5, 0.125, ((1, 8),)),
        "w_value": noise(keys[6], (D, D), D ** -0.5, 0.125, ((1, 8),)),
        "b_value": noise(keys[7], (D,), 0.02, 0.125, ((0, 8),), jnp.float32),
        "w_out": noise(keys[8], (D, D), (max(D // 256, 1)) ** -0.5, 2.0, ((0, 8),)),
        "b_out": noise(keys[9], (D,), 0.5, 3.0, (), jnp.float32),
        "ln2_gain": jnp.clip(1.0 + 0.1 * jax.random.normal(keys[10], (D,), jnp.float32), 0.5, 1.5),
        "ln2_bias": noise(keys[11], (D,), 0.3, 1.75, (), jnp.float32),
        "w_up": noise(keys[12], (D, FF), D ** -0.5, 0.125, ((1, 8),)),
        "b_up": noise(keys[13], (FF,), 0.5, 3.0, ((0, 8),), jnp.float32),
        "w_down": noise(keys[14], (FF, D), FF ** -0.5, 0.0625, ((0, 8),)),
        "b_down": noise(keys[15], (D,), 0.5, 3.0, (), jnp.float32),
        "cotangent": noise(keys[16], (TOKENS, D), 1.0, 6.0, ((0, 32),)),
        "seq_ids": draw_seq_ids(jax.random.fold_in(keys[20], 71), 0),
        "block_mask": draw_block_mask(jax.random.fold_in(keys[20], 71), 0),
        "counts": draw_counts(jax.random.fold_in(keys[20], 71), 0),
    }


epsilon = 1e-05
highest = lax.Precision.HIGHEST

@jax.custom_vjp
def low(v):
    return lax.optimization_barrier(v.astype(jnp.bfloat16)).astype(jnp.float32)

@jax.custom_vjp
def low_back(v):
    return v

def low_keep(v):
    return (low(v), None)

def low_pass(kept, grad):
    return (grad,)

def back_keep(v):
    return (v, None)

def back_low(kept, grad):
    return (low(grad),)
low.defvjp(low_keep, low_pass)
low_back.defvjp(back_keep, back_low)

def layer_norm(values, gain, bias):
    average = lax.optimization_barrier(jnp.mean(values, axis=-1, keepdims=True))
    centered = values - average
    variance = lax.optimization_barrier(jnp.mean(centered * centered, axis=-1, keepdims=True))
    return centered * lax.rsqrt(variance + epsilon) * gain + bias

def matmul(left, right):
    return jnp.dot(left, right, precision=highest)

def allowed_rows(offset, number, seq_row, mask_table):
    query_pos = offset + jnp.arange(number, dtype=jnp.int32)
    key_pos = jnp.arange(TOK_GROUP, dtype=jnp.int32)
    query_seq = lax.dynamic_slice_in_dim(seq_row, offset, number)
    table_rows = lax.dynamic_slice_in_dim(mask_table, offset // BLOCK, number // BLOCK, 0)
    spread = jnp.broadcast_to(table_rows[:, None, :, None], (number // BLOCK, BLOCK, TOK_GROUP // BLOCK, BLOCK)).reshape(number, TOK_GROUP)
    return (key_pos[None, :] <= query_pos[:, None]) & (query_seq[:, None] == seq_row[None, :]) & (spread == 1)

def attend(queries, key_rows, values, seq_row, mask_table):
    span = min(512, TOK_GROUP)
    scaling = HD ** (-0.5)

    def one_block(block_index):
        offset = (block_index * span).astype(jnp.int32)
        query_block = lax.dynamic_slice_in_dim(queries, offset, span, 0)
        scores = low_back(jnp.einsum('qhd,khd->hqk', query_block, key_rows, precision=highest) * scaling)
        allowed = allowed_rows(offset, span, seq_row, mask_table)
        scores = jnp.where(allowed[None], scores, -1e+30)
        weights = low(jax.nn.softmax(scores, axis=-1))
        return jnp.einsum('hqk,khd->qhd', weights, values, precision=highest)
    blocks = lax.map(jax.checkpoint(one_block), jnp.arange(TOK_GROUP // span, dtype=jnp.int32))
    return blocks.reshape(TOK_GROUP, HEADS * HD)

def layer(inputs, ln1_gain, ln1_bias, w_query, b_query, w_key, w_value, b_value, w_out, b_out, ln2_gain, ln2_bias, w_up, b_up, w_down, b_down, seq_row, mask_table):
    normed_one = low(layer_norm(inputs, ln1_gain, ln1_bias))
    queries = low(low_back(matmul(normed_one, w_query) + b_query))
    key_rows = low(low_back(matmul(normed_one, w_key)))
    values = low(low_back(matmul(normed_one, w_value) + b_value))
    shape = (TOK_GROUP, HEADS, HD)
    attended = attend(queries.reshape(shape), key_rows.reshape(shape), values.reshape(shape), seq_row, mask_table)
    attended = low(low_back(attended))
    middle = inputs + low_back(matmul(attended, w_out)) + b_out
    normed_two = low(layer_norm(middle, ln2_gain, ln2_bias))
    hidden = low_back(matmul(normed_two, w_up) + b_up)
    activated = low(jax.nn.gelu(hidden, approximate=True))
    return middle + low_back(matmul(activated, w_down)) + b_down

def reference(tokens, ln1_gain, ln1_bias, w_query, b_query, w_key, w_value, b_value, w_out, b_out, ln2_gain, ln2_bias, w_up, b_up, w_down, b_down, cotangent, seq_ids, block_mask, counts):
    params = tuple((weight_arg.astype(jnp.float32) for weight_arg in (ln1_gain, ln1_bias, w_query, b_query, w_key, w_value, b_value, w_out, b_out, ln2_gain, ln2_bias, w_up, b_up, w_down, b_down)))
    count_float = counts.astype(jnp.float32)
    weighting = N_DP * count_float / jnp.sum(count_float)
    inputs = tokens.astype(jnp.float32).reshape(N_DP, TOK_GROUP, D)
    cot_rows = cotangent.astype(jnp.float32).reshape(N_DP, TOK_GROUP, D)

    def one_group(carry, slices):
        x_group, cot_group, seq_row, mask_table, count_here, weight_here = slices
        valid_rows = (jnp.arange(TOK_GROUP, dtype=jnp.int32) < count_here).astype(jnp.float32)

        def forward(x_in, *weights):
            return layer(x_in, *weights, seq_row, mask_table)
        result, pull = jax.vjp(forward, x_group, *params)
        grads = pull(cot_group * valid_rows[:, None] * weight_here)
        carry = tuple((total + piece for total, piece in zip(carry, grads[1:])))
        return (carry, (result, grads[0]))
    start_sums = tuple((jnp.zeros_like(weight_arg) for weight_arg in params))
    sums, (results, grad_rows) = lax.scan(one_group, start_sums, (inputs, cot_rows, seq_ids, block_mask, counts, weighting))
    return (results.reshape(TOKENS, D), grad_rows.reshape(TOKENS, D), sums[0], sums[1], sums[2], sums[3], sums[4], sums[5], sums[6], sums[7], sums[8], sums[9], sums[10], sums[11], sums[12], sums[13], sums[14])
```

```python
import functools

import jax
import jax.numpy as jnp
from jax import lax
from jax.experimental import pallas as pl
from jax.experimental.pallas import tpu as pltpu
from jax.sharding import PartitionSpec as P

HD = 128
BLOCK = 256
SCALE = HD**-0.5
NEG = -1e30
epsilon = 1e-05
F32 = jnp.float32
BF16 = jnp.bfloat16


def norm_stats(values):
    average = jnp.mean(values, axis=-1, keepdims=True)
    centered = values - average
    variance = jnp.mean(centered * centered, axis=-1, keepdims=True)
    inverse = lax.rsqrt(variance + epsilon)
    return centered * inverse, inverse


def norm_back(normed, inverse, gain, cot):
    dn = cot * gain
    first = jnp.mean(dn, axis=-1, keepdims=True)
    second = jnp.mean(dn * normed, axis=-1, keepdims=True)
    return (dn - first - normed * second) * inverse


def dot(left, right):
    return jnp.dot(left, right, preferred_element_type=F32)


def inner_rows(left, right):
    return lax.dot_general(left, right, (((0,), (0,)), ((), ())), preferred_element_type=F32)


def times_transpose(left, right):
    return lax.dot_general(left, right, (((1,), (1,)), ((), ())), preferred_element_type=F32)


def attend_kernel(active, qkv, q_seq, k_seq, out, out_float, log_total, scores, top):
    blocks = pl.num_programs(1)
    here = pl.program_id(1)
    start = pl.multiple_of(here * BLOCK, BLOCK)
    query = qkv[pl.ds(start, BLOCK), :HD]
    row_seq = q_seq[...]
    rows = lax.broadcasted_iota(jnp.int32, (BLOCK, BLOCK), 0)
    cols = lax.broadcasted_iota(jnp.int32, (BLOCK, BLOCK), 1)
    top[...] = jnp.full((BLOCK, 1), NEG, F32)
    count = qkv.shape[0] // BLOCK
    for j in range(count):

        @pl.when(active[here * blocks + j] == 1)
        def _(j=j):
            part = times_transpose(query, qkv[j * BLOCK : (j + 1) * BLOCK, HD : 2 * HD])
            allow = (row_seq == k_seq[:, j * BLOCK : (j + 1) * BLOCK]) & (
                (cols <= rows) | (here != j)
            )
            part = jnp.where(allow, part * SCALE, NEG)
            scores[:, j * BLOCK : (j + 1) * BLOCK] = part
            top[...] = jnp.maximum(top[...], jnp.max(part, axis=-1, keepdims=True))

    biggest = top[...]
    out_float[...] = jnp.zeros((BLOCK, HD), F32)
    top[...] = jnp.zeros((BLOCK, 1), F32)
    for j in range(count):

        @pl.when(active[here * blocks + j] == 1)
        def _(j=j):
            part = jnp.exp(scores[:, j * BLOCK : (j + 1) * BLOCK] - biggest)
            top[...] += jnp.sum(part, axis=-1, keepdims=True)
            out_float[...] += dot(part.astype(BF16), qkv[j * BLOCK : (j + 1) * BLOCK, 2 * HD :])

    total = top[...]
    final = out_float[...] / total
    out_float[...] = final
    out[...] = final.astype(BF16)
    column = jnp.broadcast_to(biggest + jnp.log(total), (BLOCK, HD))
    log_total[0] = column.T[:8]


def attend(qkv, active, q_seq, k_seq):
    rows, width = qkv.shape
    heads = width // (3 * HD)
    blocks = rows // BLOCK
    grid_spec = pltpu.PrefetchScalarGridSpec(
        num_scalar_prefetch=1,
        grid=(heads, blocks),
        in_specs=[
            pl.BlockSpec((rows, 3 * HD), lambda h, i, a: (0, h)),
            pl.BlockSpec((BLOCK, 1), lambda h, i, a: (i, 0)),
            pl.BlockSpec((1, rows), lambda h, i, a: (0, 0)),
        ],
        out_specs=[
            pl.BlockSpec((BLOCK, HD), lambda h, i, a: (i, h)),
            pl.BlockSpec((BLOCK, HD), lambda h, i, a: (i, h)),
            pl.BlockSpec((1, 8, BLOCK), lambda h, i, a: (h, 0, i)),
        ],
        scratch_shapes=[pltpu.VMEM((BLOCK, rows), F32), pltpu.VMEM((BLOCK, 1), F32)],
    )
    return pl.pallas_call(
        attend_kernel,
        grid_spec=grid_spec,
        out_shape=[
            jax.ShapeDtypeStruct((rows, heads * HD), BF16),
            jax.ShapeDtypeStruct((rows, heads * HD), F32),
            jax.ShapeDtypeStruct((heads, 8, rows), F32),
        ],
        cost_estimate=pl.CostEstimate(
            flops=2 * heads * rows * rows * HD,
            bytes_accessed=rows * width * 4,
            transcendentals=heads * rows * rows // 2,
        ),
        name="attend",
    )(active, qkv, q_seq, k_seq)


def attend_back_kernel(
    active, qkv, cot, out_float, log_total, k_seq_col, q_seq_row, grad, key_acc, value_acc, query_acc
):
    blocks = pl.num_programs(1)
    here = pl.program_id(1)
    count = qkv.shape[0] // BLOCK
    start = pl.multiple_of(here * BLOCK, BLOCK)

    @pl.when(here == 0)
    def _():
        key_acc[...] = jnp.zeros(key_acc.shape, F32)
        value_acc[...] = jnp.zeros(value_acc.shape, F32)

    query = qkv[pl.ds(start, BLOCK), :HD]
    cot_here = cot[...]
    centre = jnp.sum(cot_here.astype(F32) * out_float[...], axis=-1, keepdims=True)
    centre = jnp.broadcast_to(centre, (BLOCK, HD)).T[:1]
    log_row = log_total[0, :1]
    row_seq = q_seq_row[...]
    keys = lax.broadcasted_iota(jnp.int32, (BLOCK, BLOCK), 0)
    queries = lax.broadcasted_iota(jnp.int32, (BLOCK, BLOCK), 1)
    query_acc[...] = jnp.zeros((BLOCK, HD), F32)
    for j in range(count):

        @pl.when(active[here * blocks + j] == 1)
        def _(j=j):
            spot = slice(j * BLOCK, (j + 1) * BLOCK)
            key = qkv[spot, HD : 2 * HD]
            part = times_transpose(key, query)
            allow = (k_seq_col[spot, :] == row_seq) & ((keys <= queries) | (here != j))
            weight = jnp.where(allow, jnp.exp(part * SCALE - log_row), 0.0)
            weight_cot = times_transpose(qkv[spot, 2 * HD :], cot_here)
            score_cot = (weight * (weight_cot - centre)).astype(BF16)
            value_acc[spot, :] += dot(weight.astype(BF16), cot_here)
            key_acc[spot, :] += dot(score_cot, query)
            query_acc[...] += inner_rows(score_cot, key)

    grad[pl.ds(start, BLOCK), :HD] = (query_acc[...] * SCALE).astype(BF16)

    @pl.when(here == blocks - 1)
    def _():
        grad[:, HD : 2 * HD] = (key_acc[...] * SCALE).astype(BF16)
        grad[:, 2 * HD :] = value_acc[...].astype(BF16)


def attend_back(qkv, cot, out_float, log_total, active, k_seq_col, q_seq_row):
    rows, width = qkv.shape
    heads = width // (3 * HD)
    blocks = rows // BLOCK
    grid_spec = pltpu.PrefetchScalarGridSpec(
        num_scalar_prefetch=1,
        grid=(heads, blocks),
        in_specs=[
            pl.BlockSpec((rows, 3 * HD), lambda h, i, a: (0, h)),
            pl.BlockSpec((BLOCK, HD), lambda h, i, a: (i, h)),
            pl.BlockSpec((BLOCK, HD), lambda h, i, a: (i, h)),
            pl.BlockSpec((1, 8, BLOCK), lambda h, i, a: (h, 0, i)),
            pl.BlockSpec((rows, 1), lambda h, i, a: (0, 0)),
            pl.BlockSpec((1, BLOCK), lambda h, i, a: (0, i)),
        ],
        out_specs=pl.BlockSpec((rows, 3 * HD), lambda h, i, a: (0, h)),
        scratch_shapes=[
            pltpu.VMEM((rows, HD), F32),
            pltpu.VMEM((rows, HD), F32),
            pltpu.VMEM((BLOCK, HD), F32),
        ],
    )
    return pl.pallas_call(
        attend_back_kernel,
        grid_spec=grid_spec,
        out_shape=jax.ShapeDtypeStruct((rows, width), BF16),
        cost_estimate=pl.CostEstimate(
            flops=5 * heads * rows * rows * HD,
            bytes_accessed=rows * width * 6,
            transcendentals=heads * rows * rows // 2,
        ),
        name="attend_back",
    )(active, qkv, cot, out_float, log_total, k_seq_col, q_seq_row)


class Line:
    def __init__(self):
        self.length = lax.axis_size("mp") // 2
        place = lax.axis_index("mp")
        self.chip = place // 2
        self.core = place % 2
        size = self.length
        self.order = []
        for z in range(size):
            side = 1 if z < size // 2 else -1
            others = [d for d in range(-z, size - z) if d != 0]
            others.sort(key=lambda d: (abs(d), -d * side))
            self.order.append([z] + [z + d for d in others])

    def chips(self):
        return jnp.asarray(self.order, jnp.int32)[self.chip]

    def pairs(self, links):
        return [(2 * a + c, 2 * b + c) for a, b in links for c in range(2)]

    def move(self, value, links):
        return lax.ppermute(value, "mp", self.pairs(links))

    def swap(self, value):
        return lax.ppermute(value, "mp", [(m, m ^ 1) for m in range(2 * self.length)])

    def choose(self, by_chip):
        groups = []
        for z, value in enumerate(by_chip):
            if value is None:
                continue
            for entry in groups:
                if entry[0] is value:
                    entry[1].append(z)
                    break
            else:
                groups.append((value, [z]))
        result = groups[0][0]
        for value, where in groups[1:]:
            hit = functools.reduce(jnp.logical_or, [self.chip == z for z in where])
            result = jnp.where(hit, value, result)
        return result

    def pair(self, mine):
        other = self.swap(mine)
        first = self.core == 0
        return jnp.concatenate(
            [jnp.where(first, mine, other), jnp.where(first, other, mine)], axis=0
        )

    def gather(self, mine):
        size = self.length
        right, left = [mine], [mine]
        slots = [self.pair(mine)]
        for k in range(1, size):
            if k == size - 1 and size > 2:
                value = jnp.where(self.chip < size // 2, left[-1], right[-1])
                got = self.move(value, [(size - 2, size - 1), (1, 0)])
                right.append(got)
                left.append(got)
            else:
                right.append(self.move(right[-1], [(i, i + 1) for i in range(k - 1, size - 1)]))
                left.append(self.move(left[-1], [(i, i - 1) for i in range(1, size - k + 1)]))
            source = []
            for z in range(size):
                d = self.order[z][k] - z
                source.append(left[d] if d > 0 else right[-d])
            slots.append(self.pair(self.choose(source)))
        return slots

    def scatter(self, parts):
        size = self.length
        rows = parts[0].shape[0] // 2
        first = self.core == 0
        sums = []
        for part in parts:
            low, high = part[:rows], part[rows:]
            other = self.swap(jnp.where(first, high, low))
            sums.append(
                (jnp.where(first, low, high).astype(F32) + other.astype(F32)).astype(BF16)
            )
        spot = [{chip: k for k, chip in enumerate(row)} for row in self.order]
        from_left = from_right = None
        for k in range(size - 1, 0, -1):
            go_right = [
                sums[spot[z][z + k]] if z + k < size else None for z in range(size)
            ]
            go_left = [sums[spot[z][z - k]] if z >= k else None for z in range(size)]
            if 2 * k > size - 1:
                both = [r if r is not None else m for r, m in zip(go_right, go_left)]
                value = self.choose(both)
                if from_left is not None:
                    came = from_left
                    if from_right is not from_left:
                        came = jnp.where(self.chip < size // 2, from_left, from_right)
                    value = (value.astype(F32) + came.astype(F32)).astype(BF16)
                send_right = send_left = value
            else:
                send_right = (self.choose(go_right).astype(F32) + from_left.astype(F32)).astype(BF16)
                send_left = (self.choose(go_left).astype(F32) + from_right.astype(F32)).astype(BF16)
            to_right = [(i, i + 1) for i in range(size - k)]
            to_left = [(i, i - 1) for i in range(k, size)]
            if k == size - 1 and size > 2:
                from_left = from_right = self.move(send_right, to_right + to_left)
            else:
                from_left = self.move(send_right, to_right)
                from_right = self.move(send_left, to_left)
        return sums[0].astype(F32) + from_left.astype(F32) + from_right.astype(F32)


def sum_over_dp(value):
    size = lax.axis_size("dp")
    index = lax.axis_index("dp")
    bits = size.bit_length() - 1
    half = value.shape[0] // 2
    pieces = []
    for piece, order in (
        (value[:half], list(range(bits))),
        (value[half:], list(range(bits))[::-1]),
    ):
        for b in order:
            links = [(i, i ^ (1 << b)) for i in range(size)]
            mid = piece.shape[0] // 2
            low_side = ((index >> b) & 1) == 0
            keep = jnp.where(low_side, piece[:mid], piece[mid:])
            send = jnp.where(low_side, piece[mid:], piece[:mid])
            came = lax.ppermute(send, "dp", links)
            piece = (keep.astype(F32) + came.astype(F32)).astype(BF16)
        for b in order[::-1]:
            links = [(i, i ^ (1 << b)) for i in range(size)]
            low_side = ((index >> b) & 1) == 0
            came = lax.ppermute(piece, "dp", links)
            piece = jnp.concatenate(
                [jnp.where(low_side, piece, came), jnp.where(low_side, came, piece)], axis=0
            )
        pieces.append(piece)
    return jnp.concatenate(pieces, axis=0).astype(F32)


def after(value, *others):
    return lax.optimization_barrier((value, *others))[0]


ROOT = 0.7978845608028654
CUBE = 0.044715


def gelu_and_slope(point):
    inside = jnp.tanh(ROOT * (point + CUBE * point * point * point))
    value = 0.5 * point * (1.0 + inside)
    slope = 0.5 * (1.0 + inside) + 0.5 * point * (1.0 - inside * inside) * ROOT * (
        1.0 + 3.0 * CUBE * point * point
    )
    return value, slope


def on_device(
    tokens,
    ln1_gain,
    ln1_bias,
    w_query,
    b_query,
    w_key,
    w_value,
    b_value,
    w_out,
    b_out,
    ln2_gain,
    ln2_bias,
    w_up,
    b_up,
    w_down,
    b_down,
    cotangent,
    seq_ids,
    block_mask,
    counts,
):
    rows = tokens.shape[0]
    line = Line()
    size = line.length
    both = 2 * rows
    group = both * size
    width = w_query.shape[1]
    heads = width // HD
    mp_size = lax.axis_size("mp")
    place = lax.axis_index("mp")
    chips = line.chips()

    cut = [slice(h * HD, (h + 1) * HD) for h in range(heads)]
    w_qkv = jnp.concatenate([w[:, s] for s in cut for w in (w_query, w_key, w_value)], axis=1)
    nothing = jnp.zeros_like(b_query)
    b_qkv = jnp.concatenate([b[s] for s in cut for b in (b_query, nothing, b_value)])

    blocks = group // BLOCK
    per_chip = both // BLOCK
    seq_slots = seq_ids[0].reshape(size, both)[chips]
    seq_flat = seq_slots.reshape(group)
    block_ids = (chips[:, None] * per_chip + jnp.arange(per_chip, dtype=jnp.int32)).reshape(blocks)
    in_blocks = seq_flat.reshape(blocks, BLOCK)
    low, high = jnp.min(in_blocks, axis=1), jnp.max(in_blocks, axis=1)
    mask = block_mask[0][block_ids][:, block_ids]
    active = (
        (mask == 1)
        & (block_ids[None, :] <= block_ids[:, None])
        & (low[None, :] <= high[:, None])
        & (low[:, None] <= high[None, :])
    )
    active = active.astype(jnp.int32).reshape(blocks * blocks)
    seq_column, seq_row = seq_flat[:, None], seq_flat[None, :]

    dp_size = counts.shape[0]
    count_float = counts.astype(F32)
    is_here = jnp.arange(dp_size, dtype=jnp.int32) == lax.axis_index("dp")
    count_here = jnp.sum(jnp.where(is_here, counts, 0))
    weighting = dp_size * jnp.sum(jnp.where(is_here, count_float, 0.0)) / jnp.sum(count_float)
    positions = place * rows + jnp.arange(rows, dtype=jnp.int32)
    valid_rows = (positions < count_here).astype(F32)
    out_cot = cotangent.astype(F32) * valid_rows[:, None] * weighting
    grad_down_bias = jnp.sum(out_cot, axis=0)

    inputs = tokens.astype(F32)
    normed_one, inverse_one = norm_stats(inputs)
    first = (normed_one * ln1_gain + ln1_bias).astype(BF16)
    slots_one = line.gather(first)
    qkv = jnp.concatenate(
        [(dot(slot, w_qkv) + b_qkv).astype(BF16) for slot in slots_one], axis=0
    )
    out_low = after(out_cot.astype(BF16), slots_one[-1])
    gathered_cot = lax.all_gather(out_low, "mp", axis=0, tiled=True)
    attended, attended_float, log_total = attend(qkv, active, seq_column, seq_row)
    branch = line.scatter(
        [dot(attended[k * both : (k + 1) * both], w_out).astype(BF16) for k in range(size)]
    )
    activated_cot = times_transpose(gathered_cot, w_down)
    middle = inputs + branch + b_out
    normed_two, inverse_two = norm_stats(middle)
    second = (normed_two * ln2_gain + ln2_bias).astype(BF16)
    slots_two = line.gather(second)

    activated_slots, hidden_cots, parts_two = [], [], []
    for k in range(size):
        hidden = dot(slots_two[k], w_up) + b_up
        value, slope = gelu_and_slope(hidden)
        cot_here = lax.dynamic_slice_in_dim(activated_cot, chips[k] * both, both, 0)
        activated_slots.append(value.astype(BF16))
        hidden_cots.append((cot_here * slope).astype(BF16))
        parts_two.append(times_transpose(hidden_cots[k], w_up).astype(BF16))
    normed_two_cot = line.scatter(parts_two)
    activated = jnp.zeros((group, w_up.shape[1]), BF16)
    for k in range(size):
        activated = lax.dynamic_update_slice_in_dim(
            activated, activated_slots[k], chips[k] * both, 0
        )
    last = lax.psum_scatter(
        dot(activated, w_down).astype(BF16), "mp", scatter_dimension=0, tiled=True
    )
    result = middle + last.astype(F32) + b_down
    hidden_cot = jnp.concatenate(hidden_cots, axis=0)
    grad_down = inner_rows(activated, gathered_cot).astype(BF16)
    grad_up = inner_rows(jnp.concatenate(slots_two, axis=0), hidden_cot).astype(BF16)
    grad_up_bias = jnp.sum(hidden_cot, axis=0, dtype=F32)

    grad_gain_two = jnp.sum(normed_two_cot * normed_two, axis=0)
    grad_bias_two = jnp.sum(normed_two_cot, axis=0)
    middle_cot = out_cot + norm_back(normed_two, inverse_two, ln2_gain, normed_two_cot)
    grad_out_bias = jnp.sum(middle_cot, axis=0)
    slots_three = line.gather(middle_cot.astype(BF16))
    attended_cot = jnp.concatenate(
        [times_transpose(slot, w_out).astype(BF16) for slot in slots_three], axis=0
    )
    grad_out = inner_rows(attended, jnp.concatenate(slots_three, axis=0)).astype(BF16)

    cot_qkv = attend_back(
        qkv, attended_cot, attended_float, log_total, active, seq_column, seq_row
    )
    normed_one_cot = line.scatter(
        [
            times_transpose(cot_qkv[k * both : (k + 1) * both], w_qkv).astype(BF16)
            for k in range(size)
        ]
    )
    grad_qkv = inner_rows(jnp.concatenate(slots_one, axis=0), cot_qkv).astype(BF16)
    grad_qkv_bias = jnp.sum(cot_qkv, axis=0, dtype=F32)
    grad_input = middle_cot + norm_back(normed_one, inverse_one, ln1_gain, normed_one_cot)
    grad_gain_one = jnp.sum(normed_one_cot * normed_one, axis=0)
    grad_bias_one = jnp.sum(normed_one_cot, axis=0)

    sum_down = sum_over_dp(grad_down)
    sum_up = sum_over_dp(grad_up)
    sum_out = sum_over_dp(grad_out)
    sum_qkv = sum_over_dp(grad_qkv)

    biases = jnp.concatenate([grad_qkv_bias, grad_up_bias])
    spread = jnp.where(
        jnp.arange(mp_size, dtype=jnp.int32)[:, None] == place, biases[None, :], 0.0
    )
    small, spread = lax.psum(
        (
            jnp.stack(
                [
                    grad_gain_one,
                    grad_bias_one,
                    grad_out_bias,
                    grad_gain_two,
                    grad_bias_two,
                    grad_down_bias,
                ]
            ),
            spread,
        ),
        ("dp", "mp"),
    )
    biases = lax.dynamic_index_in_dim(spread, place, 0, keepdims=False)

    def columns(array, which):
        return jnp.concatenate(
            [
                array[..., (3 * h + which) * HD : (3 * h + which + 1) * HD]
                for h in range(heads)
            ],
            axis=-1,
        )

    return (
        result,
        grad_input,
        small[0],
        small[1],
        columns(sum_qkv, 0),
        columns(biases[: 3 * width], 0),
        columns(sum_qkv, 1),
        columns(sum_qkv, 2),
        columns(biases[: 3 * width], 2),
        sum_out,
        small[2],
        small[3],
        small[4],
        sum_up,
        biases[3 * width :],
        sum_down,
        small[5],
    )


def solution(mesh):
    rows = P(("dp", "mp"), None)
    wide = P(None, "mp")
    tall = P("mp", None)
    return jax.shard_map(
        on_device,
        mesh=mesh,
        in_specs=(
            rows,
            P(),
            P(),
            wide,
            P("mp"),
            wide,
            wide,
            P("mp"),
            tall,
            P(),
            P(),
            P(),
            wide,
            P("mp"),
            tall,
            P(),
            rows,
            P("dp", None),
            P("dp", None, None),
            P(),
        ),
        out_specs=(
            rows,
            rows,
            P(),
            P(),
            wide,
            P("mp"),
            wide,
            wide,
            P("mp"),
            tall,
            P(),
            P(),
            P(),
            wide,
            P("mp"),
            tall,
            P(),
        ),
        check_vma=False,
    )
```
